32 devices in a mesh: section: 4 (over z), seq: 4 (over y, x), tp: 2 (over core).
Axes of the slice: x: 2, y: 2, z: 4, core: 2. Of those that a mesh axis runs over, the one named last changes fastest.
Arguments:
- queries: bfloat16 [4, 1024, 8192], P('section', 'seq', 'tp'), may hold values from -300 to 300
- vision: bfloat16 [128, 7680], P(('section', 'tp'), 'seq'), may hold values from -6 to 6
- kv_weight: bfloat16 [4, 7680, 2048], P('section', 'seq', 'tp'), may hold values from -0.0625 to 0.0625
- key_gain: float32 [4, 128], P('section'), may hold values from 0.25 to 1.75
- head_gate: float32 [4, 64], P('section', 'tp'), may hold values from -1.5 to 1.5
Outputs:
- attended: bfloat16 [4, 1024, 8192], P('section', 'seq', 'tp')
The draws below stay inside these ranges and needn't reach their ends.
All inputs are finite; a program needn't handle non-finite values.
Results may differ from the reference program's by a relative error of at most 0.01.
The reference program's roundings to bfloat16 on the way count: a program that leaves them out, or rounds other values in their place, can miss the bound.
Values may be sent and summed in bfloat16 or wider, within the bound.
A program may use at most 64 MiB of HBM per device.

```python
import jax
import jax.numpy as jnp
from jax import lax

DV = 7680
QH = 64
KVH = 8
HD = 128
SECTIONS = 4
TOKENS = 1024
V = 128


def draw_queries(key, part):
    base = jax.random.normal(key, (SECTIONS, TOKENS, QH * HD), jnp.float32)
    return jnp.clip(base, -6.0, 6.0).astype(jnp.bfloat16)


def steps_of(rng, dims, cuts, least, largest):
    factor_of, own = 1.0, jax.random.fold_in(rng, 6)
    for dim, shards_of in cuts:
        steps = jnp.exp(jax.random.uniform(jax.random.fold_in(own, dim), (shards_of,), jnp.float32, least / len(cuts), largest / len(cuts)))
        factor_of = factor_of * jnp.repeat(steps, dims[dim] // shards_of).reshape([-1 if axis == dim else 1 for axis in range(len(dims))])
    return factor_of


def noise(own_key, dims, width, most, pieces=(), kind=jnp.bfloat16):
    result = jax.random.normal(own_key, dims, jnp.float32) * width
    if len(pieces) > 0:
        result = steps_of(own_key, dims, pieces, -0.22, 0.18) * result
    return jnp.clip(result, min=-most, max=most).astype(kind)


def setup_inputs(seed: int = 0) -> dict:
    seeds = jax.random.split(jax.random.key(seed), 6)
    queries = draw_queries(jax.random.fold_in(seeds[5], 71), 0)
    vision = noise(seeds[1], (V, DV), 1.0, 6.0, ((0, 8), (1, 4)))
    kv_weight = noise(seeds[2], (SECTIONS, DV, KVH * 2 * HD), DV ** -0.5, 0.0625, ((0, 4), (1, 4), (2, 2)))
    key_gain = jnp.clip(1.0 + 0.15 * jax.random.normal(seeds[3], (SECTIONS, HD), jnp.float32), 0.25, 1.75)
    head_gate = jnp.clip(jax.random.uniform(seeds[4], (SECTIONS, QH), jnp.float32, -1.5, 1.5) * steps_of(seeds[4], (SECTIONS, QH), ((0, 4), (1, 2)), -0.4, 0.0), -1.5, 1.5)
    return {"queries": queries, "vision": vision, "kv_weight": kv_weight, "key_gain": key_gain, "head_gate": head_gate}


eps_norm = 1e-05

def key_values(vision, weights, gain):
    projected = jnp.dot(vision, weights, preferred_element_type=jnp.float32)
    rows = projected.shape[0]
    projected = projected.reshape(rows, KVH, 2, HD)
    keys_raw = projected[:, :, 0]
    values_raw = projected[:, :, 1]
    scaled = keys_raw * lax.rsqrt(lax.optimization_barrier(jnp.mean(keys_raw * keys_raw, axis=-1, keepdims=True)) + eps_norm) * gain
    return (scaled.astype(jnp.bfloat16), values_raw.astype(jnp.bfloat16))

def reference(queries, vision, kv_weight, key_gain, head_gate):
    group = QH // KVH

    def one_section(index):
        keys, values = key_values(vision, kv_weight[index], key_gain[index])
        grouped = queries[index].reshape(TOKENS, KVH, group, HD)

        def one_head(head):
            query_head = lax.dynamic_index_in_dim(grouped, head, 1, keepdims=False).astype(jnp.float32)
            key_head = lax.dynamic_index_in_dim(keys, head, 1, keepdims=False).astype(jnp.float32)
            value_head = lax.dynamic_index_in_dim(values, head, 1, keepdims=False).astype(jnp.float32)
            scores = jnp.einsum('tgd,rd->tgr', query_head, key_head, precision=lax.Precision.HIGHEST) * HD ** (-0.5)
            peak = lax.optimization_barrier(jnp.max(scores, axis=-1, keepdims=True))
            exp_scores = jnp.exp(scores - peak)
            total = lax.optimization_barrier(jnp.sum(exp_scores, axis=-1))
            rounded = lax.optimization_barrier(exp_scores.astype(jnp.bfloat16)).astype(jnp.float32)
            mixed = jnp.einsum('tgr,rd->tgd', rounded, value_head, precision=lax.Precision.HIGHEST)
            return mixed / total[..., None]
        heads = lax.map(one_head, jnp.arange(KVH, dtype=jnp.int32))
        heads = jnp.transpose(heads, (1, 0, 2, 3))
        gated = heads * jnp.tanh(head_gate[index]).reshape(1, KVH, group, 1)
        return gated.reshape(TOKENS, QH * HD).astype(jnp.bfloat16)
    return lax.map(one_section, jnp.arange(SECTIONS, dtype=jnp.int32))
```

```python
import functools

import jax
import jax.numpy as jnp
from jax import lax
from jax.experimental import pallas as pl
from jax.experimental.pallas import tpu as pltpu
from jax.sharding import PartitionSpec as P

MESH = pl.DeviceIdType.MESH
eps_norm = 1e-05


def project_kernel(
    sizes,
    head_dim,
    vision_ref,
    weight_ref,
    gain_ref,
    out_ref,
    seen,
    weights,
    partial,
    landed,
    ready,
    gathered,
    weight_sem,
    far_send,
    pass_send,
    seen_sem,
    sum_send,
    sum_recv,
    kv_send,
    kv_recv,
):
    n_s, n_q, n_t = sizes
    s, q, t = lax.axis_index("section"), lax.axis_index("seq"), lax.axis_index("tp")
    stages = partial.shape[0]
    half = n_s // stages
    share = partial.shape[2]
    columns = partial.shape[3]
    base = (s // half) * half

    load = pltpu.make_async_copy(weight_ref.at[0], weights, weight_sem)
    load.start()

    def section_of(stage, j):
        return lax.rem(base + stage * half, n_s) + lax.rem(s + j, half)

    others_s = [section_of(k // half, k % half) for k in range(1, n_s)]
    others_q = [lax.rem(q + k, n_q) for k in range(1, n_q)]
    others_t = [lax.rem(t + k, n_t) for k in range(1, n_t)]

    barrier = pltpu.get_barrier_semaphore()
    peers = (
        [(s, q, o) for o in others_t]
        + [(o, q, t) for o in others_s]
        + [(s, o, t) for o in others_q]
    )
    for peer in peers:
        pl.semaphore_signal(barrier, inc=1, device_id=peer, device_id_type=MESH)
    pl.semaphore_wait(barrier, len(peers))

    mine = s * n_t + t
    sent = []

    def send(src, dst, send_sem, recv_sem, peer):
        copy = pltpu.make_async_remote_copy(
            src_ref=src,
            dst_ref=dst,
            send_sem=send_sem,
            recv_sem=recv_sem,
            device_id=peer,
            device_id_type=MESH,
        )
        copy.start()
        sent.append(copy)

    def arrived(dst, sem):
        pltpu.make_async_copy(dst, dst, sem).wait()

    for k, o in enumerate(others_t):
        send(vision_ref, seen.at[mine], pass_send.at[k], seen_sem.at[mine], (s, q, o))
    for k, o in enumerate(others_s):
        send(vision_ref, seen.at[mine], far_send.at[k], seen_sem.at[mine], (o, q, t))
    seen[mine] = vision_ref[...]
    load.wait()

    for stage in range(stages):
        first = lax.rem(base + stage * half, n_s)
        for j in range(half):
            o = section_of(stage, j)
            slot = o * n_t + t
            if stage * half + j > 0:
                arrived(seen.at[slot], seen_sem.at[slot])
                for k, p in enumerate(others_t):
                    send(
                        seen.at[slot],
                        seen.at[slot],
                        pass_send.at[(stage * half + j) * (n_t - 1) + k],
                        seen_sem.at[slot],
                        (s, q, p),
                    )
        for j in range(half):
            o = section_of(stage, j)
            for p in others_t:
                slot = o * n_t + p
                arrived(seen.at[slot], seen_sem.at[slot])
        block = seen[pl.ds(first * n_t, half * n_t)]
        block = block.reshape(block.shape[0] * block.shape[1], block.shape[2])
        width = 2 * head_dim
        for c in range(columns // width):
            at = slice(c * width, (c + 1) * width)
            product = jnp.dot(block, weights[:, at], preferred_element_type=jnp.float32)
            partial[stage, :, :, at] = product.reshape(n_q, share, width)
        for k, o in enumerate(others_q):
            send(
                partial.at[stage, o],
                landed.at[stage, k],
                sum_send.at[stage, k],
                sum_recv.at[stage, k],
                (s, o, t),
            )

    for stage in range(stages):
        for k in range(n_q - 1):
            arrived(landed.at[stage, k], sum_recv.at[stage, k])
        for h in range(columns // (2 * head_dim)):
            at_k = slice(2 * h * head_dim, (2 * h + 1) * head_dim)
            at_v = slice((2 * h + 1) * head_dim, (2 * h + 2) * head_dim)
            raw_k = partial[stage, q, :, at_k]
            raw_v = partial[stage, q, :, at_v]
            for k in range(n_q - 1):
                raw_k += landed[stage, k, :, at_k]
                raw_v += landed[stage, k, :, at_v]
            mean = jnp.mean(raw_k * raw_k, axis=-1, keepdims=True)
            scaled = raw_k * lax.rsqrt(mean + eps_norm) * gain_ref[...]
            ready[stage, :, at_k] = scaled.astype(jnp.bfloat16)
            ready[stage, :, at_v] = raw_v.astype(jnp.bfloat16)
        for k, o in enumerate(others_q):
            send(
                ready.at[stage],
                gathered.at[stage, q],
                kv_send.at[stage, k],
                kv_recv.at[stage, q],
                (s, o, t),
            )
        gathered[stage, q] = ready[stage]

    for stage in range(stages):
        for o in others_q:
            arrived(gathered.at[stage, o], kv_recv.at[stage, o])
    out_ref[...] = gathered[...].reshape(out_ref.shape)
    for copy in sent:
        copy.wait_send()


def attend_kernel(head_dim, group, pair, q_ref, kv_ref, gate_ref, out_ref):
    head = pl.program_id(0)
    keys = kv_ref[:, :head_dim]
    values = kv_ref[:, head_dim:]
    rows = keys.shape[0]
    tokens = q_ref.shape[1]
    scale = head_dim ** (-0.5)
    if pair == 2:
        zero = jnp.zeros_like(keys)
        keys = jnp.concatenate(
            [jnp.concatenate([keys, zero], 1), jnp.concatenate([zero, keys], 1)], 0
        )
        values = jnp.concatenate(
            [jnp.concatenate([values, zero], 1), jnp.concatenate([zero, values], 1)], 0
        )
    for g in range(0, group, pair):
        at = slice(g * head_dim, (g + pair) * head_dim)
        scores = lax.dot_general(
            q_ref[0, :, at], keys, (((1,), (1,)), ((), ())), preferred_element_type=jnp.float32
        )
        exps, factors = [], []
        for p in range(pair):
            part = scores[:, p * rows : (p + 1) * rows]
            peak = jnp.max(part, axis=-1, keepdims=True)
            exp_scores = jnp.exp((part - peak) * scale)
            total = jnp.sum(exp_scores, axis=-1, keepdims=True)
            gate = jnp.tanh(jnp.full((1, head_dim), gate_ref[0, head * group + g + p]))
            factors.append(gate / jnp.broadcast_to(total, (tokens, head_dim)))
            exps.append(exp_scores.astype(jnp.bfloat16))
        exps = exps[0] if pair == 1 else jnp.concatenate(exps, 1)
        factors = factors[0] if pair == 1 else jnp.concatenate(factors, 1)
        mixed = jnp.dot(exps, values, preferred_element_type=jnp.float32)
        out_ref[0, :, at] = (mixed * factors).astype(jnp.bfloat16)


def local(sizes, queries, vision, kv_weight, key_gain, head_gate):
    n_s, n_q, n_t = sizes
    head_dim = key_gain.shape[1]
    shard, features = vision.shape
    columns = kv_weight.shape[2]
    rows = shard * n_s * n_t
    stages = 2 if n_s % 2 == 0 and rows % (32 * n_q) == 0 else 1
    share = rows // (stages * n_q)
    vmem = pl.BlockSpec(memory_space=pltpu.VMEM)
    dma = pltpu.SemaphoreType.DMA
    key_values = pl.pallas_call(
        functools.partial(project_kernel, sizes, head_dim),
        out_shape=jax.ShapeDtypeStruct((rows, columns), jnp.bfloat16),
        in_specs=[vmem, pl.BlockSpec(memory_space=pl.ANY), vmem],
        out_specs=vmem,
        scratch_shapes=[
            pltpu.VMEM((n_s * n_t, shard, features), jnp.bfloat16),
            pltpu.VMEM((features, columns), jnp.bfloat16),
            pltpu.VMEM((stages, n_q, share, columns), jnp.float32),
            pltpu.VMEM((stages, n_q - 1, share, columns), jnp.float32),
            pltpu.VMEM((stages, share, columns), jnp.bfloat16),
            pltpu.VMEM((stages, n_q, share, columns), jnp.bfloat16),
            dma,
            dma((n_s - 1,)),
            dma((n_s * (n_t - 1),)),
            dma((n_s * n_t,)),
            dma((stages, n_q - 1)),
            dma((stages, n_q - 1)),
            dma((stages, n_q - 1)),
            dma((stages, n_q)),
        ],
        compiler_params=pltpu.CompilerParams(collective_id=0, has_side_effects=True),
        name="project",
    )(vision, kv_weight, key_gain)

    tokens = queries.shape[1]
    pair_heads = columns // (2 * head_dim)
    group = head_gate.shape[1] // pair_heads
    pair = 2 if group % 2 == 0 and rows == head_dim else 1
    wide = group * head_dim
    return pl.pallas_call(
        functools.partial(attend_kernel, head_dim, group, pair),
        out_shape=jax.ShapeDtypeStruct(queries.shape, jnp.bfloat16),
        grid=(pair_heads,),
        in_specs=[
            pl.BlockSpec((1, tokens, wide), lambda i: (0, 0, i)),
            pl.BlockSpec((rows, 2 * head_dim), lambda i: (0, i)),
            pl.BlockSpec(memory_space=pltpu.SMEM),
        ],
        out_specs=pl.BlockSpec((1, tokens, wide), lambda i: (0, 0, i)),
        name="attend",
    )(queries, key_values, head_gate)


def solution(mesh):
    sizes = tuple(mesh.shape[name] for name in ("section", "seq", "tp"))
    return jax.shard_map(
        functools.partial(local, sizes),
        mesh=mesh,
        in_specs=(
            P("section", "seq", "tp"),
            P(("section", "tp"), "seq"),
            P("section", "seq", "tp"),
            P("section", None),
            P("section", "tp"),
        ),
        out_specs=P("section", "seq", "tp"),
        check_vma=False,
    )
```

```python
import functools

import jax
import jax.numpy as jnp
from jax import lax
from jax.experimental import pallas as pl
from jax.experimental.pallas import tpu as pltpu
from jax.sharding import PartitionSpec as P

MESH = pl.DeviceIdType.MESH
eps_norm = 1e-05


def project_kernel(
    sizes,
    head_dim,
    vision_ref,
    weight_ref,
    gain_ref,
    query_ref,
    key_ref,
    value_ref,
    staged_ref,
    seen,
    weights,
    gain,
    partial,
    landed,
    ready,
    gathered,
    load_sem,
    far_send,
    pass_send,
    seen_sem,
    sum_send,
    sum_recv,
    kv_send,
    kv_recv,
):
    n_s, n_q, n_t = sizes
    s, q, t = lax.axis_index("section"), lax.axis_index("seq"), lax.axis_index("tp")
    stages = partial.shape[0]
    per = n_s // stages
    half = n_s // 2 if n_s % 2 == 0 else n_s
    share = partial.shape[2]
    columns = partial.shape[3]
    heads = columns // (2 * head_dim)
    base = (s // half) * half

    def section_of(k):
        return lax.rem(base + (k // half) * half, n_s) + lax.rem(s + k, half)

    def place_at(k):
        return (k // half) * half + (half - k % half) % half

    others_s = [section_of(k) for k in range(1, n_s)]
    others_q = [lax.rem(q + k, n_q) for k in range(1, n_q)]
    others_t = [lax.rem(t + k, n_t) for k in range(1, n_t)]

    barrier = pltpu.get_barrier_semaphore()
    peers = (
        [(o, q, t) for o in others_s[::-1]]
        + [(s, o, t) for o in others_q]
        + [(s, q, o) for o in others_t]
    )
    for peer in peers:
        pl.semaphore_signal(barrier, inc=1, device_id=peer, device_id_type=MESH)
    own = pltpu.make_async_copy(vision_ref, seen.at[0, t], load_sem.at[0])
    own.start()
    load = pltpu.make_async_copy(weight_ref.at[0], weights, load_sem.at[1])
    load.start()
    load_gain = pltpu.make_async_copy(gain_ref, gain, load_sem.at[2])
    load_gain.start()
    stage_queries = pltpu.make_async_copy(query_ref, staged_ref, load_sem.at[3])
    stage_queries.start()
    own.wait()
    pl.semaphore_wait(barrier, len(peers))

    sent = []

    def send(src, dst, send_sem, recv_sem, peer):
        copy = pltpu.make_async_remote_copy(
            src_ref=src,
            dst_ref=dst,
            send_sem=send_sem,
            recv_sem=recv_sem,
            device_id=peer,
            device_id_type=MESH,
        )
        copy.start()
        sent.append(copy)

    def arrived(dst, sem):
        pltpu.make_async_copy(dst, dst, sem).wait()

    def pass_on(k):
        for i, o in enumerate(others_t):
            send(seen.at[k, t], seen.at[k, t], pass_send.at[k, i], seen_sem.at[k, t], (s, q, o))

    pass_on(0)
    for k, o in enumerate(others_s, 1):
        place = place_at(k)
        send(
            seen.at[0, t], seen.at[place, t], far_send.at[k - 1], seen_sem.at[place, t], (o, q, t)
        )
    load_gain.wait()
    load.wait()

    def project(stage):
        for k in range(stage * per, (stage + 1) * per):
            if k > 0:
                arrived(seen.at[k, t], seen_sem.at[k, t])
                pass_on(k)
        for k in range(stage * per, (stage + 1) * per):
            for o in others_t:
                arrived(seen.at[k, o], seen_sem.at[k, o])
        block = seen[stage * per : (stage + 1) * per]
        block = block.reshape(n_q * share, block.shape[3])
        width = 2 * head_dim
        for h in range(heads):
            at = slice(h * width, (h + 1) * width)
            product = jnp.dot(block, weights[:, at], preferred_element_type=jnp.float32)
            partial[stage, :, :, at] = product.reshape(n_q, share, width)
        for k, o in enumerate(others_q):
            send(
                partial.at[stage, o],
                landed.at[stage, k],
                sum_send.at[stage, k],
                sum_recv.at[stage, k],
                (s, o, t),
            )

    def finish(stage):
        for k in range(n_q - 1):
            arrived(landed.at[stage, k], sum_recv.at[stage, k])
        for h in range(heads):
            at_k = slice(2 * h * head_dim, (2 * h + 1) * head_dim)
            at_v = slice((2 * h + 1) * head_dim, (2 * h + 2) * head_dim)
            raw_k = partial[stage, q, :, at_k]
            raw_v = partial[stage, q, :, at_v]
            for k in range(n_q - 1):
                raw_k += landed[stage, k, :, at_k]
                raw_v += landed[stage, k, :, at_v]
            mean = jnp.mean(raw_k * raw_k, axis=-1, keepdims=True)
            scaled = raw_k * lax.rsqrt(mean + eps_norm) * gain[...]
            both = jnp.concatenate([scaled, raw_v], axis=0).astype(jnp.bfloat16)
            ready[stage, :, h * head_dim : (h + 1) * head_dim] = both
        for k, o in enumerate(others_q):
            send(
                ready.at[stage],
                gathered.at[stage, q],
                kv_send.at[stage, k],
                kv_recv.at[stage, q],
                (s, o, t),
            )
        gathered[stage, q] = ready[stage]

    def collect(stage):
        for o in others_q:
            arrived(gathered.at[stage, o], kv_recv.at[stage, o])
        block = gathered[stage].astype(jnp.float32)
        at = slice(stage * n_q * share, (stage + 1) * n_q * share)
        shape = (n_q * share, heads * head_dim)
        key_ref[at, :] = block[:, :share].reshape(shape).astype(jnp.bfloat16)
        value_ref[at, :] = block[:, share:].reshape(shape).astype(jnp.bfloat16)

    for stage in range(stages):
        project(stage)
        if stage >= 2:
            finish(stage - 2)
    for stage in range(max(stages - 2, 0), stages):
        finish(stage)
    for stage in range(stages):
        collect(stage)
    stage_queries.wait()
    for copy in sent:
        copy.wait_send()


def attend_kernel(head_dim, group, pair, q_ref, k_ref, v_ref, gate_ref, out_ref):
    head = pl.program_id(0)
    at_head = pl.ds(pl.multiple_of(head * head_dim, head_dim), head_dim)
    keys = k_ref[:, at_head]
    values = v_ref[:, at_head]
    rows = keys.shape[0]
    scale = head_dim ** (-0.5)
    ones = jnp.ones((rows, head_dim), jnp.bfloat16)

    def diagonal(block):
        if pair == 1:
            return block
        zero = jnp.zeros_like(block)
        return jnp.concatenate(
            [jnp.concatenate([block, zero], 1), jnp.concatenate([zero, block], 1)], 0
        )

    keys, values, ones = diagonal(keys), diagonal(values), diagonal(ones)
    wide = pair * head_dim
    tokens = q_ref.shape[1]
    tile = tokens // 1
    units = [(g, r) for g in range(0, group, pair) for r in range(0, tokens, tile)]

    def score(g, r):
        start = pl.multiple_of(head * (group * head_dim) + g * head_dim, wide)
        return lax.dot_general(
            q_ref[0, r : r + tile, pl.ds(start, wide)],
            keys,
            (((1,), (1,)), ((), ())),
            preferred_element_type=jnp.float32,
        )

    def soften(scores):
        exps = []
        for p in range(pair):
            part = scores[:, p * rows : (p + 1) * rows]
            peak = jnp.max(part, axis=-1, keepdims=True)
            exps.append(jnp.exp((part - peak) * scale).astype(jnp.bfloat16))
        return exps[0] if pair == 1 else jnp.concatenate(exps, 1)

    def mix(exps, g, r):
        gates = [
            jnp.full((1, head_dim), gate_ref[0, head * group + g + p]) for p in range(pair)
        ]
        gates = gates[0] if pair == 1 else jnp.concatenate(gates, 1)
        mixed = jnp.dot(exps, values, preferred_element_type=jnp.float32)
        total = jnp.dot(exps, ones, preferred_element_type=jnp.float32)
        result = mixed / total * jnp.tanh(gates)
        out_ref[0, r : r + tile, g * head_dim : g * head_dim + wide] = result.astype(jnp.bfloat16)

    depth = 1
    waiting_scores, waiting_exps = [], []
    for step in range(len(units) + 2 * depth):
        if step < len(units):
            waiting_scores.append(score(*units[step]))
        if depth <= step < len(units) + depth:
            waiting_exps.append(soften(waiting_scores.pop(0)))
        if step >= 2 * depth:
            mix(waiting_exps.pop(0), *units[step - 2 * depth])


def local(sizes, queries, vision, kv_weight, key_gain, head_gate):
    n_s, n_q, n_t = sizes
    head_dim = key_gain.shape[1]
    shard, features = vision.shape
    columns = kv_weight.shape[2]
    rows = shard * n_s * n_t
    stages = 1
    for tried in (2, 4):
        if n_s % tried == 0 and rows % (tried * 8 * n_q) == 0:
            stages = tried
    share = rows // (stages * n_q)
    hbm = pl.BlockSpec(memory_space=pltpu.HBM)
    vmem = pl.BlockSpec(memory_space=pltpu.VMEM)
    dma = pltpu.SemaphoreType.DMA
    keys, values, staged = pl.pallas_call(
        functools.partial(project_kernel, sizes, head_dim),
        out_shape=(
            pltpu.VMEM((rows, columns // 2), jnp.bfloat16),
            pltpu.VMEM((rows, columns // 2), jnp.bfloat16),
            pltpu.VMEM(queries.shape, jnp.bfloat16),
        ),
        in_specs=[hbm, hbm, hbm, hbm],
        out_specs=(vmem, vmem, vmem),
        scratch_shapes=[
            pltpu.VMEM((n_s, n_t, shard, features), jnp.bfloat16),
            pltpu.VMEM((features, columns), jnp.bfloat16),
            pltpu.VMEM(key_gain.shape, jnp.float32),
            pltpu.VMEM((stages, n_q, share, columns), jnp.float32),
            pltpu.VMEM((stages, n_q - 1, share, columns), jnp.float32),
            pltpu.VMEM((stages, 2 * share, columns // 2), jnp.bfloat16),
            pltpu.VMEM((stages, n_q, 2 * share, columns // 2), jnp.bfloat16),
            dma((4,)),
            dma((n_s - 1,)),
            dma((n_s, n_t - 1)),
            dma((n_s, n_t)),
            dma((stages, n_q - 1)),
            dma((stages, n_q - 1)),
            dma((stages, n_q - 1)),
            dma((stages, n_q)),
        ],
        compiler_params=pltpu.CompilerParams(
            collective_id=0, has_side_effects=True, vmem_limit_bytes=24 << 20
        ),
        name="project",
    )(*[pltpu.with_memory_space_constraint(x, pltpu.HBM) for x in (vision, kv_weight, key_gain, queries)])

    tokens = queries.shape[1]
    pair_heads = columns // (2 * head_dim)
    group = head_gate.shape[1] // pair_heads
    pair = 2 if group % 2 == 0 and rows == head_dim else 1
    wide = group * head_dim
    return pl.pallas_call(
        functools.partial(attend_kernel, head_dim, group, pair),
        out_shape=jax.ShapeDtypeStruct(queries.shape, jnp.bfloat16),
        grid=(pair_heads,),
        in_specs=[vmem, vmem, vmem, pl.BlockSpec(memory_space=pltpu.SMEM)],
        out_specs=pl.BlockSpec((1, tokens, wide), lambda i: (0, 0, i)),
        compiler_params=pltpu.CompilerParams(vmem_limit_bytes=24 << 20),
        name="attend",
    )(staged, keys, values, head_gate)


def solution(mesh):
    sizes = tuple(mesh.shape[name] for name in ("section", "seq", "tp"))
    return jax.shard_map(
        functools.partial(local, sizes),
        mesh=mesh,
        in_specs=(
            P("section", "seq", "tp"),
            P(("section", "tp"), "seq"),
            P("section", "seq", "tp"),
            P("section", None),
            P("section", "tp"),
        ),
        out_specs=P("section", "seq", "tp"),
        check_vma=False,
    )
```

```python
import functools

import jax
import jax.numpy as jnp
from jax import lax
from jax.experimental import pallas as pl
from jax.experimental.pallas import tpu as pltpu
from jax.sharding import PartitionSpec as P

MESH = pl.DeviceIdType.MESH
eps_norm = 1e-05


def project_kernel(
    sizes,
    head_dim,
    vision_ref,
    weight_ref,
    gain_ref,
    query_ref,
    key_ref,
    value_ref,
    staged_ref,
    seen,
    weights,
    gain,
    partial,
    landed,
    ready,
    gathered,
    load_sem,
    far_send,
    pass_send,
    seen_sem,
    sum_send,
    sum_recv,
    kv_send,
    kv_recv,
):
    n_s, n_q, n_t = sizes
    s, q, t = lax.axis_index("section"), lax.axis_index("seq"), lax.axis_index("tp")
    stages = partial.shape[0]
    per = n_s // stages
    half = n_s // 2 if n_s % 2 == 0 else n_s
    share = partial.shape[2]
    columns = partial.shape[3]
    heads = columns // (2 * head_dim)
    base = (s // half) * half

    def section_of(k):
        return lax.rem(base + (k // half) * half, n_s) + lax.rem(s + k, half)

    def place_at(k):
        return (k // half) * half + (half - k % half) % half

    others_s = [section_of(k) for k in range(1, n_s)]
    others_q = [lax.rem(q + k, n_q) for k in range(1, n_q)]
    others_t = [lax.rem(t + k, n_t) for k in range(1, n_t)]

    barrier = pltpu.get_barrier_semaphore()
    peers = (
        [(o, q, t) for o in others_s[::-1]]
        + [(s, o, t) for o in others_q]
        + [(s, q, o) for o in others_t]
    )
    for peer in peers:
        pl.semaphore_signal(barrier, inc=1, device_id=peer, device_id_type=MESH)
    own = pltpu.make_async_copy(vision_ref, seen.at[0, t], load_sem.at[0])
    own.start()
    load = pltpu.make_async_copy(weight_ref.at[0], weights, load_sem.at[1])
    load.start()
    load_gain = pltpu.make_async_copy(gain_ref, gain, load_sem.at[2])
    load_gain.start()
    stage_queries = pltpu.make_async_copy(query_ref, staged_ref, load_sem.at[3])
    stage_queries.start()
    own.wait()
    pl.semaphore_wait(barrier, len(peers))

    sent = []

    def send(src, dst, send_sem, recv_sem, peer):
        copy = pltpu.make_async_remote_copy(
            src_ref=src,
            dst_ref=dst,
            send_sem=send_sem,
            recv_sem=recv_sem,
            device_id=peer,
            device_id_type=MESH,
        )
        copy.start()
        sent.append(copy)

    def arrived(dst, sem):
        pltpu.make_async_copy(dst, dst, sem).wait()

    def pass_on(k):
        for i, o in enumerate(others_t):
            send(seen.at[k, t], seen.at[k, t], pass_send.at[k, i], seen_sem.at[k, t], (s, q, o))

    pass_on(0)
    for k, o in enumerate(others_s, 1):
        place = place_at(k)
        send(
            seen.at[0, t], seen.at[place, t], far_send.at[k - 1], seen_sem.at[place, t], (o, q, t)
        )
    load_gain.wait()
    load.wait()

    def project(stage):
        for k in range(stage * per, (stage + 1) * per):
            if k > 0:
                arrived(seen.at[k, t], seen_sem.at[k, t])
                pass_on(k)
        for k in range(stage * per, (stage + 1) * per):
            for o in others_t:
                arrived(seen.at[k, o], seen_sem.at[k, o])
        block = seen[stage * per : (stage + 1) * per]
        block = block.reshape(n_q * share, block.shape[3])
        width = 2 * head_dim
        for h in range(heads):
            at = slice(h * width, (h + 1) * width)
            product = jnp.dot(block, weights[:, at], preferred_element_type=jnp.float32)
            partial[stage, :, :, at] = product.reshape(n_q, share, width)
        for k, o in enumerate(others_q):
            send(
                partial.at[stage, o],
                landed.at[stage, k],
                sum_send.at[stage, k],
                sum_recv.at[stage, k],
                (s, o, t),
            )

    def finish(stage):
        for k in range(n_q - 1):
            arrived(landed.at[stage, k], sum_recv.at[stage, k])
        for h in range(heads):
            at_k = slice(2 * h * head_dim, (2 * h + 1) * head_dim)
            at_v = slice((2 * h + 1) * head_dim, (2 * h + 2) * head_dim)
            raw_k = partial[stage, q, :, at_k]
            raw_v = partial[stage, q, :, at_v]
            for k in range(n_q - 1):
                raw_k += landed[stage, k, :, at_k]
                raw_v += landed[stage, k, :, at_v]
            mean = jnp.mean(raw_k * raw_k, axis=-1, keepdims=True)
            scaled = raw_k * lax.rsqrt(mean + eps_norm) * gain[...]
            both = jnp.concatenate([scaled, raw_v], axis=0).astype(jnp.bfloat16)
            ready[stage, :, h * head_dim : (h + 1) * head_dim] = both
        for k, o in enumerate(others_q):
            send(
                ready.at[stage],
                gathered.at[stage, q],
                kv_send.at[stage, k],
                kv_recv.at[stage, q],
                (s, o, t),
            )
        gathered[stage, q] = ready[stage]

    def collect(stage):
        for o in others_q:
            arrived(gathered.at[stage, o], kv_recv.at[stage, o])
        block = gathered[stage].astype(jnp.float32)
        at = slice(stage * n_q * share, (stage + 1) * n_q * share)
        shape = (n_q * share, heads * head_dim)
        key_ref[at, :] = block[:, :share].reshape(shape).astype(jnp.bfloat16)
        value_ref[at, :] = block[:, share:].reshape(shape).astype(jnp.bfloat16)

    for stage in range(stages):
        project(stage)
        if stage >= 2:
            finish(stage - 2)
    for stage in range(max(stages - 2, 0), stages):
        finish(stage)
    for stage in range(stages):
        collect(stage)
    stage_queries.wait()
    for copy in sent:
        copy.wait_send()


def attend_kernel(head_dim, group, pair, many, q_ref, k_ref, v_ref, gate_ref, out_ref):
    first = pl.program_id(0) * many
    rows = k_ref.shape[0]
    scale = head_dim ** (-0.5)
    ones = jnp.ones((rows, head_dim), jnp.bfloat16)

    def diagonal(block):
        if pair == 1:
            return block
        zero = jnp.zeros_like(block)
        return jnp.concatenate(
            [jnp.concatenate([block, zero], 1), jnp.concatenate([zero, block], 1)], 0
        )

    keys, values, ones = [], [], diagonal(ones)
    for i in range(many):
        at = pl.ds(pl.multiple_of((first + i) * head_dim, head_dim), head_dim)
        keys.append(diagonal(k_ref[:, at]))
        values.append(diagonal(v_ref[:, at]))
    wide = pair * head_dim
    tokens = q_ref.shape[1]
    tile = tokens // 1
    units = [(g, r) for g in range(0, many * group, pair) for r in range(0, tokens, tile)]

    def score(g, r):
        start = pl.multiple_of(first * (group * head_dim) + g * head_dim, wide)
        return lax.dot_general(
            q_ref[0, r : r + tile, pl.ds(start, wide)],
            keys[g // group],
            (((1,), (1,)), ((), ())),
            preferred_element_type=jnp.float32,
        )

    def soften(scores):
        exps = []
        for p in range(pair):
            part = scores[:, p * rows : (p + 1) * rows]
            peak = jnp.max(part, axis=-1, keepdims=True)
            exps.append(jnp.exp((part - peak) * scale).astype(jnp.bfloat16))
        return exps[0] if pair == 1 else jnp.concatenate(exps, 1)

    def mix(exps, g, r):
        gates = [
            jnp.full((1, head_dim), gate_ref[0, first * group + g + p]) for p in range(pair)
        ]
        gates = gates[0] if pair == 1 else jnp.concatenate(gates, 1)
        mixed = jnp.dot(exps, values[g // group], preferred_element_type=jnp.float32)
        total = jnp.dot(exps, ones, preferred_element_type=jnp.float32)
        result = mixed / total * jnp.tanh(gates)
        out_ref[0, r : r + tile, g * head_dim : g * head_dim + wide] = result.astype(jnp.bfloat16)

    depth = 2
    waiting_scores, waiting_exps = [], []
    for step in range(len(units) + 2 * depth):
        if step < len(units):
            waiting_scores.append(score(*units[step]))
        if depth <= step < len(units) + depth:
            waiting_exps.append(soften(waiting_scores.pop(0)))
        if step >= 2 * depth:
            mix(waiting_exps.pop(0), *units[step - 2 * depth])


def local(sizes, queries, vision, kv_weight, key_gain, head_gate):
    n_s, n_q, n_t = sizes
    head_dim = key_gain.shape[1]
    shard, features = vision.shape
    columns = kv_weight.shape[2]
    rows = shard * n_s * n_t
    stages = 1
    for tried in (2, 4):
        if n_s % tried == 0 and rows % (tried * 8 * n_q) == 0:
            stages = tried
    share = rows // (stages * n_q)
    hbm = pl.BlockSpec(memory_space=pltpu.HBM)
    vmem = pl.BlockSpec(memory_space=pltpu.VMEM)
    dma = pltpu.SemaphoreType.DMA
    keys, values, staged = pl.pallas_call(
        functools.partial(project_kernel, sizes, head_dim),
        out_shape=(
            pltpu.VMEM((rows, columns // 2), jnp.bfloat16),
            pltpu.VMEM((rows, columns // 2), jnp.bfloat16),
            pltpu.VMEM(queries.shape, jnp.bfloat16),
        ),
        in_specs=[hbm, hbm, hbm, hbm],
        out_specs=(vmem, vmem, vmem),
        scratch_shapes=[
            pltpu.VMEM((n_s, n_t, shard, features), jnp.bfloat16),
            pltpu.VMEM((features, columns), jnp.bfloat16),
            pltpu.VMEM(key_gain.shape, jnp.float32),
            pltpu.VMEM((stages, n_q, share, columns), jnp.float32),
            pltpu.VMEM((stages, n_q - 1, share, columns), jnp.float32),
            pltpu.VMEM((stages, 2 * share, columns // 2), jnp.bfloat16),
            pltpu.VMEM((stages, n_q, 2 * share, columns // 2), jnp.bfloat16),
            dma((4,)),
            dma((n_s - 1,)),
            dma((n_s, n_t - 1)),
            dma((n_s, n_t)),
            dma((stages, n_q - 1)),
            dma((stages, n_q - 1)),
            dma((stages, n_q - 1)),
            dma((stages, n_q)),
        ],
        compiler_params=pltpu.CompilerParams(
            collective_id=0, has_side_effects=True, vmem_limit_bytes=24 << 20
        ),
        name="project",
    )(*[pltpu.with_memory_space_constraint(x, pltpu.HBM) for x in (vision, kv_weight, key_gain, queries)])

    tokens = queries.shape[1]
    pair_heads = columns // (2 * head_dim)
    group = head_gate.shape[1] // pair_heads
    pair = 2 if group % 2 == 0 and rows == head_dim else 1
    many = 2 if pair_heads % 4 == 0 else 1
    wide = many * group * head_dim
    return pl.pallas_call(
        functools.partial(attend_kernel, head_dim, group, pair, many),
        out_shape=jax.ShapeDtypeStruct(queries.shape, jnp.bfloat16),
        grid=(pair_heads // many,),
        in_specs=[vmem, vmem, vmem, pl.BlockSpec(memory_space=pltpu.SMEM)],
        out_specs=pl.BlockSpec((1, tokens, wide), lambda i: (0, 0, i)),
        compiler_params=pltpu.CompilerParams(vmem_limit_bytes=24 << 20),
        name="attend",
    )(staged, keys, values, head_gate)


def solution(mesh):
    sizes = tuple(mesh.shape[name] for name in ("section", "seq", "tp"))
    return jax.shard_map(
        functools.partial(local, sizes),
        mesh=mesh,
        in_specs=(
            P("section", "seq", "tp"),
            P(("section", "tp"), "seq"),
            P("section", "seq", "tp"),
            P("section", None),
            P("section", "tp"),
        ),
        out_specs=P("section", "seq", "tp"),
        check_vma=False,
    )
```
